32 devices in a mesh: dp: 4 (over x, core), seq: 2 (over y), tensor: 4 (over z).
Axes of the slice: x: 2, y: 2, z: 4, core: 2. Of those that a mesh axis runs over, the one named last changes fastest.
Arguments:
- tokens: bfloat16 [8, 1024, 768], P('dp', 'seq'), may hold values from -6 to 6
- segments: int32 [8, 1024], P('dp'), may hold values from 0 to 2, never falling along the last dimension, each value on 1 to 512 neighbouring positions
- projections: bfloat16 [3, 768, 768], P(None, ('dp', 'seq'), 'tensor'), may hold values from -0.21875 to 0.21875
- offsets: bfloat16 [2, 12, 64], P(None, 'tensor', ('dp', 'seq')), may hold values from -3 to 3
- mixing: bfloat16 [768, 768], P('tensor', ('dp', 'seq')), may hold values from -2.5 to 2.5
- upward: bfloat16 [768, 3072], P(('dp', 'seq'), 'tensor'), may hold values from -0.21875 to 0.21875
- thresholds: bfloat16 [48, 64], P('tensor', ('dp', 'seq')), may hold values from -3 to 3
- downward: bfloat16 [3072, 768], P('tensor', ('dp', 'seq')), may hold values from -0.109375 to 0.109375
- scales: bfloat16 [2, 768], P(None, ('dp', 'seq')), may hold values from 0.099609375 to 1.8984375
- shifts: bfloat16 [2, 768], P(None, ('dp', 'seq')), may hold values from -2 to 2
- biases: bfloat16 [2, 768], P(None, ('dp', 'seq')), may hold values from -2 to 2
- cotangent: bfloat16 [8, 1024, 768], P('dp', 'seq'), may hold values from -6 to 6
Outputs:
- result: bfloat16 [8, 1024, 768], P('dp', 'seq')
- tokens_grad: bfloat16 [8, 1024, 768], P('dp', 'seq')
- projections_grad: float32 [3, 768, 768], P(None, ('dp', 'seq'), 'tensor')
- offsets_grad: float32 [2, 12, 64], P(None, 'tensor', ('dp', 'seq'))
- mixing_grad: float32 [768, 768], P('tensor', ('dp', 'seq'))
- upward_grad: float32 [768, 3072], P(('dp', 'seq'), 'tensor')
- thresholds_grad: float32 [48, 64], P('tensor', ('dp', 'seq'))
- downward_grad: float32 [3072, 768], P('tensor', ('dp', 'seq'))
- scales_grad: float32 [2, 768], P(None, ('dp', 'seq'))
- shifts_grad: float32 [2, 768], P(None, ('dp', 'seq'))
- biases_grad: float32 [2, 768], P(None, ('dp', 'seq'))
The draws below stay inside these ranges and needn't reach their ends.
Inputs may be any that keep to these rules, and one draw needn't show every extreme that they name: `segments`: ids never fall along a sequence; each document holds 1 to 512 tokens, and one holds exactly 512.
All inputs are finite; a program needn't handle non-finite values.
Results may differ from the reference program's by a relative error of at most 0.012.
Values may be sent and summed in bfloat16 or wider, within the bound.
A program may use at most 128 MiB of HBM per device.

```python
import math
import jax
import jax.numpy as jnp
import numpy as np
from jax import lax

D = 768
HEADS = 12
HEADDIM = 64
FF = 3072
SEQLEN = 1024
SEQS = 8
DOCS = 3
DOC_MOST = 512


def shard_levels(own_key, dims, shards, smallest, top_value):
    level = 1.0
    for axis_at, shards_of in shards:
        draws = jax.random.uniform(jax.random.fold_in(jax.random.fold_in(own_key, 6), axis_at), (shards_of,), jnp.float32, smallest / len(shards), top_value / len(shards))
        level = level * jnp.repeat(jnp.exp(draws), dims[axis_at] // shards_of).reshape((-1,) + (1,) * (len(dims) - 1 - axis_at))
    return level


def split_up(number_of, total, bound, lean):
    portions = [(1 << 20) // math.isqrt(rank ** lean) + 1 for rank in range(2, number_of + 1)]
    spare, given = total - bound - (number_of - 1), [1] * (number_of - 1)
    while spare > 0:
        movable = [i for i in range(number_of - 1) if given[i] < bound]
        pool, remaining = sum([portions[i] for i in movable]), spare
        for i in movable:
            addition = min(bound - given[i], max(1, remaining * portions[i] // pool), spare)
            given[i] = given[i] + addition
            spare = spare - addition
    return np.array([bound] + given)


def uneven(key, count, total, bound, skew):
    if count == 2:
        one = jax.random.randint(key, (), max(1, total - bound), min(bound, total - 1) + 1)
        return jnp.stack([one, total - one])
    sizes = jnp.asarray(split_up(count, total, bound, skew), jnp.int32)
    pairs = (count - 1) // 2
    source_of, taker = sizes[1:1 + 2 * pairs:2], sizes[2:2 + 2 * pairs:2]
    slack = jnp.minimum(source_of - 1, bound - taker)
    shifted = jax.random.randint(jax.random.fold_in(key, 1), (pairs,), 0, 1 << 20) % (slack + 1)
    sizes = sizes.at[1:1 + 2 * pairs:2].set(source_of - shifted).at[2:2 + 2 * pairs:2].set(taker + shifted)
    return sizes[jax.random.permutation(jax.random.fold_in(key, 2), count)]


def centred(own_key, dims, spread, limit, split=(), kind=jnp.bfloat16):
    values = spread * jax.random.normal(own_key, dims, jnp.float32)
    if split:
        values = values * shard_levels(own_key, dims, split, -0.22, 0.18)
    return jnp.clip(values, -limit, limit).astype(kind)


def setup_inputs(seed: int = 0) -> dict:
    seeds = jax.random.split(jax.random.key(seed), 13)
    tokens = centred(seeds[0], (SEQS, SEQLEN, D), 1.0, 6.0, ((0, 4), (1, 2)))
    segments = jax.vmap(lambda own: jnp.searchsorted(jnp.cumsum(uneven(own, DOCS, SEQLEN, DOC_MOST, 1)), jnp.arange(SEQLEN), side="right"))(jax.random.split(seeds[1], SEQS)).reshape((SEQS, SEQLEN)).astype(jnp.int32)
    projections = centred(seeds[2], (3, D, D), D ** -0.5, 0.21875, ((1, 8), (2, 4)))
    offsets = centred(seeds[3], (2, HEADS, HEADDIM), 0.5, 3.0, ((1, 4), (2, 8)))
    mixing = centred(seeds[4], (D, D), (max(1, D // 128)) ** -0.5, 2.5, ((0, 4), (1, 8)))
    upward = centred(seeds[5], (D, FF), D ** -0.5, 0.21875, ((0, 8), (1, 4)))
    thresholds = centred(seeds[6], (FF // HEADDIM, HEADDIM), 0.5, 3.0, ((0, 4), (1, 8)))
    downward = centred(seeds[7], (FF, D), FF ** -0.5, 0.109375, ((0, 4), (1, 8)))
    scales = jnp.clip(1.0 + 0.18 * jax.random.normal(seeds[8], (2, D), jnp.float32), 0.099609375, 1.8984375).astype(jnp.bfloat16)
    shifts = centred(seeds[9], (2, D), 0.3, 2.0, ((1, 8),))
    biases = centred(seeds[10], (2, D), 0.3, 2.0, ((1, 8),))
    cotangent = centred(seeds[11], (SEQS, SEQLEN, D), 1.0, 6.0, ((0, 4), (1, 2)))
    return {"tokens": tokens, "segments": segments, "projections": projections, "offsets": offsets, "mixing": mixing, "upward": upward, "thresholds": thresholds, "downward": downward, "scales": scales, "shifts": shifts, "biases": biases, "cotangent": cotangent}


@jax.custom_vjp
def low(v):
    return lax.optimization_barrier(v.astype(jnp.bfloat16)).astype(jnp.float32)

@jax.custom_vjp
def low_back(v):
    return v

def low_keep(v):
    return (low(v), None)

def low_pass(kept, grad):
    return (grad,)

def back_keep(v):
    return (v, None)

def back_low(kept, grad):
    return (low(grad),)
low.defvjp(low_keep, low_pass)
low_back.defvjp(back_keep, back_low)

def norm_rows(values, gain_row, shift_row):
    average = lax.optimization_barrier(jnp.mean(values, axis=-1, keepdims=True))
    centered = values - average
    variance = lax.optimization_barrier(jnp.mean(centered * centered, axis=-1, keepdims=True))
    return centered * lax.rsqrt(variance + 1e-05) * gain_row + shift_row

def gelu_tanh(values):
    return 0.5 * values * (1.0 + jnp.tanh(0.7978845608028654 * (values + 0.044715 * values * values * values)))

def dense(left, right):
    return jnp.matmul(left, right, precision=lax.Precision.HIGHEST)

def sequence_forward(params, inputs, seg_row):
    projections, offsets, mixing, upward, thresholds, downward, scales, shifts, biases = params
    length = inputs.shape[0]
    head_count = offsets.shape[1]
    head_size = offsets.shape[2]
    normed = low(norm_rows(inputs, scales[0], shifts[0]))
    query = low(low_back(dense(normed, projections[0]) + offsets[0].reshape(-1)))
    keys = low(low_back(dense(normed, projections[1])))
    values = low(low_back(dense(normed, projections[2]) + offsets[1].reshape(-1)))
    places = jnp.arange(length, dtype=jnp.int32)
    allowed = (places[None, :] <= places[:, None]) & (seg_row[None, :] == seg_row[:, None])

    def split_heads(matrix):
        return matrix.reshape(length, head_count, head_size).transpose(1, 0, 2)

    def attend(triple):
        query_head, key_head, value_head = triple
        scores = low_back(dense(query_head, key_head.T) * 0.125)
        scores = jnp.where(allowed, scores, -1e+30)
        log_total = jax.nn.logsumexp(scores, axis=1, keepdims=True)
        probs = low(jnp.exp(scores - log_total))
        return dense(probs, value_head)
    heads_out = lax.map(jax.checkpoint(attend), (split_heads(query), split_heads(keys), split_heads(values)))
    attended = low(low_back(heads_out.transpose(1, 0, 2).reshape(length, -1)))
    hidden = inputs + low_back(dense(attended, mixing)) + biases[0]
    normed2 = low(norm_rows(hidden, scales[1], shifts[1]))
    pre_act = low_back(dense(normed2, upward) + thresholds.reshape(-1))
    activated = low(gelu_tanh(pre_act))
    return hidden + low_back(dense(activated, downward)) + biases[1]

def reference(tokens, segments, projections, offsets, mixing, upward, thresholds, downward, scales, shifts, biases, cotangent):
    weights = tuple((initial.astype(jnp.float32) for initial in (projections, offsets, mixing, upward, thresholds, downward, scales, shifts, biases)))

    def forward_all(inputs, *params):

        def one_sequence(pair):
            return sequence_forward(params, pair[0], pair[1])
        return lax.map(jax.checkpoint(one_sequence), (inputs, segments))
    result, pullback = jax.vjp(forward_all, tokens.astype(jnp.float32), *weights)
    grads = pullback(cotangent.astype(jnp.float32))
    return (result.astype(jnp.bfloat16), grads[0].astype(jnp.bfloat16), grads[1], grads[2], grads[3], grads[4], grads[5], grads[6], grads[7], grads[8], grads[9])
```

```python
import functools

import jax
import jax.numpy as jnp
from jax import lax
from jax.experimental import pallas as pl
from jax.experimental.pallas import tpu as pltpu
from jax.sharding import PartitionSpec as P

LANES = 128
SHARDS = ("dp", "seq")


def norm_stats(values):
    average = jnp.mean(values, axis=-1, keepdims=True)
    centered = values - average
    inverse = lax.rsqrt(jnp.mean(centered * centered, axis=-1, keepdims=True) + 1e-05)
    return centered * inverse, inverse


def norm_back(normal, inverse, gain_row, grad):
    scaled = grad * gain_row
    return inverse * (
        scaled
        - jnp.mean(scaled, axis=-1, keepdims=True)
        - normal * jnp.mean(scaled * normal, axis=-1, keepdims=True)
    )


def gelu_tanh(values):
    return (
        0.5
        * values
        * (1.0 + jnp.tanh(0.7978845608028654 * (values + 0.044715 * values * values * values)))
    )


def head_scores(query_head, key_head, allowed):
    scores = (
        jnp.einsum("qe,ke->qk", query_head, key_head, preferred_element_type=jnp.float32) * 0.125
    )
    return jnp.where(allowed, scores, -1e30)


def dot(equation, left, right):
    return jnp.einsum(equation, left, right, preferred_element_type=jnp.float32)


def line_sum_kernel(count, x_ref, out_ref, from_left, from_right, to_right, to_left, held, sems):
    me = lax.axis_index("tensor")
    streams = x_ref.shape[0]
    last = count - 1

    def neighbour(step):
        return {"tensor": jnp.clip(me + step, 0, last)}

    def copy(source, target, kind, stream, chunk, step):
        return pltpu.make_async_remote_copy(
            src_ref=source,
            dst_ref=target,
            send_sem=sems.at[2 * kind, stream, chunk],
            recv_sem=sems.at[2 * kind + 1, stream, chunk],
            device_id=neighbour(step),
            device_id_type=pl.DeviceIdType.MESH,
        )

    def partial(stream, owner, step, mine):
        arrived, leaving = (from_left, to_right) if step > 0 else (from_right, to_left)
        source = x_ref.at[stream, owner] if mine else leaving.at[stream, owner]
        return copy(source, arrived.at[stream, owner], 0 if step > 0 else 1, stream, owner, step)

    def total(stream, owner, step):
        place = held.at[stream, owner]
        return copy(place, place, 2 if step > 0 else 3, stream, owner, step)

    def send_partials(stream):
        for k in range(last):
            for step in (1, -1):
                owner = last - k if step > 0 else k
                arrived, leaving = (from_left, to_right) if step > 0 else (from_right, to_left)
                first = me == 0 if step > 0 else me == last
                inside = (me > 0) & (me < owner) if step > 0 else (me < last) & (me > owner)

                @pl.when(first)
                def _():
                    partial(stream, owner, step, True).start()

                @pl.when(inside)
                def _():
                    partial(stream, owner, step, False).wait_recv()
                    leaving[stream, owner] = (
                        arrived[stream, owner].astype(jnp.float32)
                        + x_ref[stream, owner].astype(jnp.float32)
                    ).astype(jnp.bfloat16)
                    partial(stream, owner, step, False).start()

    def finish(stream):
        own = x_ref[stream, pl.ds(me, 1)].astype(jnp.float32)

        @pl.when(me == 0)
        def _():
            partial(stream, me, -1, False).wait_recv()
            right = from_right[stream, pl.ds(me, 1)].astype(jnp.float32)
            held[stream, pl.ds(me, 1)] = (own + right).astype(jnp.bfloat16)

        @pl.when(me == last)
        def _():
            partial(stream, me, 1, False).wait_recv()
            left = from_left[stream, pl.ds(me, 1)].astype(jnp.float32)
            held[stream, pl.ds(me, 1)] = (own + left).astype(jnp.bfloat16)

        @pl.when((me > 0) & (me < last))
        def _():
            partial(stream, me, -1, False).wait_recv()
            partial(stream, me, 1, False).wait_recv()
            left = from_left[stream, pl.ds(me, 1)].astype(jnp.float32)
            right = from_right[stream, pl.ds(me, 1)].astype(jnp.float32)
            held[stream, pl.ds(me, 1)] = (own + left + right).astype(jnp.bfloat16)

        @pl.when(me < last)
        def _():
            total(stream, me, 1).start()

        @pl.when(me > 0)
        def _():
            total(stream, me, -1).start()

    def forward(stream):
        for k in range(1, count):
            for step in (1, -1):
                chunk = me - k if step > 0 else me + k
                comes = chunk >= 0 if step > 0 else chunk <= last
                goes = comes & (me < last) if step > 0 else comes & (me > 0)

                @pl.when(comes)
                def _():
                    total(stream, chunk, step).wait_recv()

                if k < last:

                    @pl.when(goes)
                    def _():
                        total(stream, chunk, step).start()

    barrier = pltpu.get_barrier_semaphore()
    for step in (1, -1):

        @pl.when(me < last if step > 0 else me > 0)
        def _():
            pl.semaphore_signal(
                barrier, inc=1, device_id=neighbour(step), device_id_type=pl.DeviceIdType.MESH
            )

    peers = jnp.where(me < last, 1, 0) + jnp.where(me > 0, 1, 0)
    pl.semaphore_wait(barrier, peers)

    for tick in range(streams + 2):
        if tick < streams:
            send_partials(tick)
        if 0 <= tick - 1 < streams:
            finish(tick - 1)
        if 0 <= tick - 2:
            forward(tick - 2)
            out_ref[tick - 2] = held[tick - 2]
    for stream in range(streams):
        for k in range(last):
            for step in (1, -1):
                owner = last - k if step > 0 else k

                @pl.when(me < owner if step > 0 else me > owner)
                def _():
                    partial(stream, owner, step, False).wait_send()

                chunk = me - k if step > 0 else me + k
                goes = (chunk >= 0) & (me < last) if step > 0 else (chunk <= last) & (me > 0)

                @pl.when(goes)
                def _():
                    total(stream, chunk, step).wait_send()


def tensor_sum(parts, streams, ident):
    count = lax.axis_size("tensor")
    values = jnp.concatenate([part.astype(jnp.bfloat16) for part in parts], axis=0)
    rows, width = values.shape
    shape = (streams, count, rows // (streams * count), width)
    scratch = [pltpu.VMEM(shape, jnp.bfloat16)] * 5
    summed = pl.pallas_call(
        functools.partial(line_sum_kernel, count),
        out_shape=jax.ShapeDtypeStruct(shape, jnp.bfloat16),
        in_specs=[pl.BlockSpec(memory_space=pltpu.VMEM)],
        out_specs=pl.BlockSpec(memory_space=pltpu.VMEM),
        scratch_shapes=scratch + [pltpu.SemaphoreType.DMA((8, streams, count))],
        compiler_params=pltpu.CompilerParams(collective_id=ident, has_side_effects=True),
        name="line_sum",
    )(values.reshape(shape))
    return jnp.split(summed.reshape(rows, width), len(parts), axis=0)


def pack_small(small, rows):
    columns = -(-small.shape[-1] // rows)
    padded = -(-columns // LANES) * LANES
    lead = small.shape[:-1]
    pads = [(0, 0)] * len(lead)
    filled = jnp.pad(small, pads + [(0, rows * columns - small.shape[-1])])
    filled = filled.reshape(lead + (rows, columns))
    return jnp.pad(filled, pads + [(0, 0), (0, padded - columns)])


def unpack_small(block, rows, size):
    columns = -(-size // rows)
    return block[:, :columns].reshape(-1, rows * columns)[:, :size]


def per_device(
    tokens,
    segments,
    projections,
    offsets,
    mixing,
    upward,
    thresholds,
    downward,
    scales,
    shifts,
    biases,
    cotangent,
):
    micro, block_len, width = tokens.shape
    seq_len = segments.shape[1]
    shards = lax.axis_size(SHARDS)
    heads = offsets.shape[1]
    piece = offsets.shape[2]
    head_size = piece * shards
    inner = heads * head_size
    rows = upward.shape[0]
    hidden_units = upward.shape[1]
    start = lax.axis_index("seq") * block_len
    query_pos = start + jnp.arange(block_len, dtype=jnp.int32)
    key_pos = jnp.arange(seq_len, dtype=jnp.int32)

    small = jnp.concatenate(
        [
            offsets.reshape(-1),
            thresholds.reshape(-1),
            scales.reshape(-1),
            shifts.reshape(-1),
            biases.reshape(-1),
        ]
    )
    small_size = small.shape[0]
    packed = jnp.concatenate(
        [
            upward,
            downward.T,
            mixing.T,
            projections[0],
            projections[1],
            projections[2],
            pack_small(small, rows),
        ],
        axis=1,
    )
    full = lax.all_gather(packed, SHARDS, axis=0, tiled=True)
    up = full[:, :hidden_units]
    down_t = full[:, hidden_units : 2 * hidden_units]
    mix_t = full[:, 2 * hidden_units : 2 * hidden_units + inner]
    entry = full[:, 2 * hidden_units + inner : 2 * hidden_units + 4 * inner]
    table = unpack_small(full[:, 2 * hidden_units + 4 * inner :], rows, small_size)
    table = table.astype(jnp.float32)
    cuts = [0, offsets.size, offsets.size + thresholds.size]
    offset_rows = (
        table[:, cuts[0] : cuts[1]]
        .reshape(shards, 2, heads, piece)
        .transpose(1, 2, 0, 3)
        .reshape(2, inner)
    )
    threshold_row = (
        table[:, cuts[1] : cuts[2]]
        .reshape(shards, thresholds.shape[0], thresholds.shape[1])
        .transpose(1, 0, 2)
        .reshape(-1)
    )
    norm_rows = (
        table[:, cuts[2] :].reshape(shards, 6, rows).transpose(1, 0, 2).reshape(6, shards * rows)
    )
    scale_rows, shift_rows, bias_rows = norm_rows[0:2], norm_rows[2:4], norm_rows[4:6]

    inputs = []
    normals = []
    inverses = []
    normed = []
    stacks = []
    for b in range(micro):
        value = tokens[b].astype(jnp.float32)
        normal, inverse = norm_stats(value)
        inputs.append(value)
        normals.append(normal)
        inverses.append(inverse)
        normed.append((normal * scale_rows[0] + shift_rows[0]).astype(jnp.bfloat16))
        stacks.append(dot("cd,de->ce", normed[b], entry))
    query_b = [(s[:, :inner] + offset_rows[0]).astype(jnp.bfloat16) for s in stacks]
    key_value = jnp.stack(
        [
            jnp.concatenate(
                [s[:, inner : 2 * inner], s[:, 2 * inner :] + offset_rows[1]], axis=1
            ).astype(jnp.bfloat16)
            for s in stacks
        ]
    )
    key_value_full = lax.all_gather(key_value, "seq", axis=1, tiled=True)

    allowed = []
    probs_all = []
    attended = []
    branch = []
    for b in range(micro):
        seg_row = segments[b]
        own_seg = lax.dynamic_slice_in_dim(seg_row, start, block_len)
        allowed.append(
            (key_pos[None, :] <= query_pos[:, None]) & (seg_row[None, :] == own_seg[:, None])
        )
        pieces = []
        totals = []
        for h in range(heads):
            cols = slice(h * head_size, (h + 1) * head_size)
            vcols = slice(inner + h * head_size, inner + (h + 1) * head_size)
            scores = head_scores(query_b[b][:, cols], key_value_full[b][:, cols], allowed[b])
            log_total = jax.nn.logsumexp(scores, axis=1, keepdims=True)
            weights_b = jnp.exp(scores - log_total).astype(jnp.bfloat16)
            pieces.append(dot("qk,ke->qe", weights_b, key_value_full[b][:, vcols]))
            totals.append(log_total)
        probs_all.append(totals)
        attended.append(jnp.concatenate(pieces, axis=1).astype(jnp.bfloat16))
        branch.append(dot("ce,de->cd", attended[b], mix_t))

    branch = tensor_sum(branch, 4, 0)
    hidden = []
    normals2 = []
    inverses2 = []
    normed2 = []
    pre_act = []
    activated = []
    lifted = []
    for b in range(micro):
        hidden.append(inputs[b] + branch[b].astype(jnp.float32) + bias_rows[0])
        normal, inverse = norm_stats(hidden[b])
        normals2.append(normal)
        inverses2.append(inverse)
        normed2.append((normal * scale_rows[1] + shift_rows[1]).astype(jnp.bfloat16))
        pre_act.append(dot("cd,df->cf", normed2[b], up) + threshold_row)
        activated.append(gelu_tanh(pre_act[b]).astype(jnp.bfloat16))

    grad_pre = []
    grad_sum2 = []
    for b in range(micro):
        grad_act = dot("cd,df->cf", cotangent[b], down_t)
        unused, gelu_back = jax.vjp(gelu_tanh, pre_act[b])
        grad_pre.append(gelu_back(grad_act)[0].astype(jnp.bfloat16))
        grad_sum2.append(dot("cf,df->cd", grad_pre[b], up))
    for b in range(micro):
        lifted.append(dot("cf,df->cd", activated[b], down_t))
    sums = tensor_sum(grad_sum2 + lifted, 4, 1)
    grad_sum2, lifted = sums[:micro], sums[micro:]
    results = [
        (hidden[b] + lifted[b].astype(jnp.float32) + bias_rows[1]).astype(jnp.bfloat16)
        for b in range(micro)
    ]

    both = lambda parts: jnp.concatenate(parts, axis=0)
    grad_pre_all = both(grad_pre)
    cotangent_all = cotangent.reshape(micro * block_len, width)
    threshold_grad = jnp.sum(grad_pre_all.astype(jnp.float32), axis=0)
    ffn_grads = jnp.concatenate(
        [
            dot("cd,cf->df", both(normed2), grad_pre_all).astype(jnp.bfloat16),
            dot("cd,cf->df", cotangent_all, both(activated)).astype(jnp.bfloat16),
        ],
        axis=1,
    )
    ffn_own = lax.psum_scatter(ffn_grads, SHARDS, scatter_dimension=0, tiled=True)

    grad_hidden = []
    grad_hidden_b = []
    scale2 = 0.0
    shift2 = 0.0
    query_grads = []
    key_value_grads = []
    for b in range(micro):
        grad_norm2 = grad_sum2[b].astype(jnp.float32)
        grad_hidden.append(
            cotangent[b].astype(jnp.float32)
            + norm_back(normals2[b], inverses2[b], scale_rows[1], grad_norm2)
        )
        scale2 += jnp.sum(grad_norm2 * normals2[b], axis=0)
        shift2 += jnp.sum(grad_norm2, axis=0)
        grad_hidden_b.append(grad_hidden[b].astype(jnp.bfloat16))
        grad_attended = dot("cd,de->ce", grad_hidden_b[b], mix_t).astype(jnp.bfloat16)
        grads_q = []
        grads_k = []
        grads_v = []
        for h in range(heads):
            cols = slice(h * head_size, (h + 1) * head_size)
            vcols = slice(inner + h * head_size, inner + (h + 1) * head_size)
            scores = head_scores(query_b[b][:, cols], key_value_full[b][:, cols], allowed[b])
            probs = jnp.exp(scores - probs_all[b][h])
            grad_slice = grad_attended[:, cols]
            grad_probs = dot("qe,ke->qk", grad_slice, key_value_full[b][:, vcols])
            delta = jnp.sum(probs * grad_probs, axis=1, keepdims=True)
            grad_scores = (probs * (grad_probs - delta)).astype(jnp.bfloat16)
            grads_q.append(dot("qk,ke->qe", grad_scores, key_value_full[b][:, cols]) * 0.125)
            grads_v.append(dot("qk,qe->ke", probs.astype(jnp.bfloat16), grad_slice))
            grads_k.append(dot("qk,qe->ke", grad_scores, query_b[b][:, cols]) * 0.125)
        query_grads.append(jnp.concatenate(grads_q, axis=1).astype(jnp.bfloat16))
        key_value_grads.append(jnp.concatenate(grads_k + grads_v, axis=1).astype(jnp.bfloat16))
    key_value_own = lax.psum_scatter(
        jnp.stack(key_value_grads), "seq", scatter_dimension=1, tiled=True
    )

    triples = []
    grad_normed = []
    for b in range(micro):
        triples.append(jnp.concatenate([query_grads[b], key_value_own[b]], axis=1))
        grad_normed.append(dot("ce,de->cd", triples[b], entry))
    grad_normed = tensor_sum(grad_normed, 4, 0)
    triple_all = both(triples)
    grad_hidden_all = both(grad_hidden_b)
    triple_sums = jnp.sum(triple_all.astype(jnp.float32), axis=0)
    scale1 = 0.0
    shift1 = 0.0
    bias1 = 0.0
    input_grads = []
    for b in range(micro):
        grad_norm = grad_normed[b].astype(jnp.float32)
        back = norm_back(normals[b], inverses[b], scale_rows[0], grad_norm)
        input_grads.append((grad_hidden[b] + back).astype(jnp.bfloat16))
        scale1 += jnp.sum(grad_norm * normals[b], axis=0)
        shift1 += jnp.sum(grad_norm, axis=0)
        bias1 += jnp.sum(grad_hidden[b], axis=0)
    bias2 = jnp.sum(cotangent_all.astype(jnp.float32), axis=0)

    offset_grad = jnp.stack([triple_sums[:inner], triple_sums[2 * inner :]])
    small_grads = jnp.concatenate(
        [
            offset_grad.reshape(2, heads, shards, piece).transpose(2, 0, 1, 3).reshape(shards, -1),
            threshold_grad.reshape(thresholds.shape[0], shards, thresholds.shape[1])
            .transpose(1, 0, 2)
            .reshape(shards, -1),
            jnp.stack([scale1, scale2, shift1, shift2, bias1, bias2])
            .reshape(6, shards, rows)
            .transpose(1, 0, 2)
            .reshape(shards, -1),
        ],
        axis=1,
    )
    small_block = pack_small(small_grads, rows).reshape(shards * rows, -1)
    att_grads = jnp.concatenate(
        [
            dot("cd,ce->de", grad_hidden_all, both(attended)).astype(jnp.bfloat16),
            dot("cd,ce->de", both(normed), triple_all).astype(jnp.bfloat16),
            small_block.astype(jnp.bfloat16),
        ],
        axis=1,
    )
    att_own = lax.psum_scatter(att_grads, SHARDS, scatter_dimension=0, tiled=True)
    att_own = att_own.astype(jnp.float32)
    ffn_own = ffn_own.astype(jnp.float32)
    own_small = unpack_small(att_own[:, 4 * inner :], rows, small_size)[0]
    own_norms = own_small[cuts[2] :].reshape(6, rows)
    own_entry = att_own[:, inner : 4 * inner]
    return (
        jnp.stack(results),
        jnp.stack(input_grads),
        jnp.stack([own_entry[:, t * inner : (t + 1) * inner] for t in range(3)]),
        own_small[cuts[0] : cuts[1]].reshape(offsets.shape),
        att_own[:, :inner].T,
        ffn_own[:, :hidden_units],
        own_small[cuts[1] : cuts[2]].reshape(thresholds.shape),
        ffn_own[:, hidden_units:].T,
        own_norms[0:2],
        own_norms[2:4],
        own_norms[4:6],
    )


def solution(mesh):
    placed = (
        P("dp", "seq", None),
        P("dp", None),
        P(None, ("dp", "seq"), "tensor"),
        P(None, "tensor", ("dp", "seq")),
        P("tensor", ("dp", "seq")),
        P(("dp", "seq"), "tensor"),
        P("tensor", ("dp", "seq")),
        P("tensor", ("dp", "seq")),
        P(None, ("dp", "seq")),
        P(None, ("dp", "seq")),
        P(None, ("dp", "seq")),
        P("dp", "seq", None),
    )
    return jax.shard_map(
        per_device,
        mesh=mesh,
        in_specs=placed,
        out_specs=(
            P("dp", "seq", None),
            P("dp", "seq", None),
            P(None, ("dp", "seq"), "tensor"),
            P(None, "tensor", ("dp", "seq")),
            P("tensor", ("dp", "seq")),
            P(("dp", "seq"), "tensor"),
            P("tensor", ("dp", "seq")),
            P("tensor", ("dp", "seq")),
            P(None, ("dp", "seq")),
            P(None, ("dp", "seq")),
            P(None, ("dp", "seq")),
        ),
        check_vma=False,
    )
```

```python
import functools

import jax
import jax.numpy as jnp
from jax import lax
from jax.experimental import pallas as pl
from jax.experimental.pallas import tpu as pltpu
from jax.sharding import PartitionSpec as P

LANES = 128
SHARDS = ("dp", "seq")


def norm_stats(values):
    average = jnp.mean(values, axis=-1, keepdims=True)
    centered = values - average
    inverse = lax.rsqrt(jnp.mean(centered * centered, axis=-1, keepdims=True) + 1e-05)
    return centered * inverse, inverse


def norm_back(normal, inverse, gain_row, grad):
    scaled = grad * gain_row
    return inverse * (
        scaled
        - jnp.mean(scaled, axis=-1, keepdims=True)
        - normal * jnp.mean(scaled * normal, axis=-1, keepdims=True)
    )


def gelu_tanh(values):
    return (
        0.5
        * values
        * (1.0 + jnp.tanh(0.7978845608028654 * (values + 0.044715 * values * values * values)))
    )


def head_scores(query_head, key_head, allowed):
    scores = (
        jnp.einsum("qe,ke->qk", query_head, key_head, preferred_element_type=jnp.float32) * 0.125
    )
    return jnp.where(allowed, scores, -1e30)


def dot(equation, left, right):
    return jnp.einsum(equation, left, right, preferred_element_type=jnp.float32)


def line_sum_kernel(count, x_ref, out_ref, from_left, from_right, to_right, to_left, held, sems):
    me = lax.axis_index("tensor")
    streams = x_ref.shape[0]
    last = count - 1

    def neighbour(step):
        return {"tensor": jnp.clip(me + step, 0, last)}

    def copy(source, target, kind, stream, chunk, step):
        return pltpu.make_async_remote_copy(
            src_ref=source,
            dst_ref=target,
            send_sem=sems.at[2 * kind, stream, chunk],
            recv_sem=sems.at[2 * kind + 1, stream, chunk],
            device_id=neighbour(step),
            device_id_type=pl.DeviceIdType.MESH,
        )

    def partial(stream, owner, step, mine):
        arrived, leaving = (from_left, to_right) if step > 0 else (from_right, to_left)
        source = x_ref.at[stream, owner] if mine else leaving.at[stream, owner]
        return copy(source, arrived.at[stream, owner], 0 if step > 0 else 1, stream, owner, step)

    def total(stream, owner, step):
        place = held.at[stream, owner]
        return copy(place, place, 2 if step > 0 else 3, stream, owner, step)

    def send_partials(stream, hop):
        for step in (1, -1):
            arrived, leaving = (from_left, to_right) if step > 0 else (from_right, to_left)

            @pl.when(me == hop if step > 0 else me == last - hop)
            def _():
                for k in range(last - hop):
                    owner = last - k if step > 0 else k
                    if hop > 0:
                        partial(stream, owner, step, False).wait_recv()
                        leaving[stream, owner] = (
                            arrived[stream, owner].astype(jnp.float32)
                            + x_ref[stream, owner].astype(jnp.float32)
                        ).astype(jnp.bfloat16)
                    partial(stream, owner, step, hop == 0).start()

    def finish(stream):
        own = x_ref[stream, pl.ds(me, 1)].astype(jnp.float32)

        @pl.when(me == 0)
        def _():
            partial(stream, me, -1, False).wait_recv()
            right = from_right[stream, pl.ds(me, 1)].astype(jnp.float32)
            held[stream, pl.ds(me, 1)] = (own + right).astype(jnp.bfloat16)

        @pl.when(me == last)
        def _():
            partial(stream, me, 1, False).wait_recv()
            left = from_left[stream, pl.ds(me, 1)].astype(jnp.float32)
            held[stream, pl.ds(me, 1)] = (own + left).astype(jnp.bfloat16)

        @pl.when((me > 0) & (me < last))
        def _():
            partial(stream, me, -1, False).wait_recv()
            partial(stream, me, 1, False).wait_recv()
            left = from_left[stream, pl.ds(me, 1)].astype(jnp.float32)
            right = from_right[stream, pl.ds(me, 1)].astype(jnp.float32)
            held[stream, pl.ds(me, 1)] = (own + left + right).astype(jnp.bfloat16)

        @pl.when(me < last)
        def _():
            total(stream, me, 1).start()

        @pl.when(me > 0)
        def _():
            total(stream, me, -1).start()

    def forward(stream, k):
        for step in (1, -1):
            chunk = me - k if step > 0 else me + k
            comes = chunk >= 0 if step > 0 else chunk <= last
            goes = comes & (me < last) if step > 0 else comes & (me > 0)

            @pl.when(comes)
            def _():
                total(stream, chunk, step).wait_recv()

            if k < last:

                @pl.when(goes)
                def _():
                    total(stream, chunk, step).start()

    barrier = pltpu.get_barrier_semaphore()
    for step in (1, -1):

        @pl.when(me < last if step > 0 else me > 0)
        def _():
            pl.semaphore_signal(
                barrier, inc=1, device_id=neighbour(step), device_id_type=pl.DeviceIdType.MESH
            )

    peers = jnp.where(me < last, 1, 0) + jnp.where(me > 0, 1, 0)
    pl.semaphore_wait(barrier, peers)

    for tick in range(streams + 2 * last):
        for hop in range(last):
            if 0 <= tick - hop < streams:
                send_partials(tick - hop, hop)
        if 0 <= tick - last < streams:
            finish(tick - last)
        for k in range(1, count):
            if 0 <= tick - last - k < streams:
                forward(tick - last - k, k)
        if 0 <= tick - 2 * last < streams:
            out_ref[tick - 2 * last] = held[tick - 2 * last]
    for stream in range(streams):
        for k in range(last):
            for step in (1, -1):
                owner = last - k if step > 0 else k

                @pl.when(me < owner if step > 0 else me > owner)
                def _():
                    partial(stream, owner, step, False).wait_send()

                chunk = me - k if step > 0 else me + k
                goes = (chunk >= 0) & (me < last) if step > 0 else (chunk <= last) & (me > 0)

                @pl.when(goes)
                def _():
                    total(stream, chunk, step).wait_send()


def tensor_sum(parts, streams, ident):
    count = lax.axis_size("tensor")
    values = jnp.concatenate([part.astype(jnp.bfloat16) for part in parts], axis=0)
    rows, width = values.shape
    shape = (streams, count, rows // (streams * count), width)
    scratch = [pltpu.VMEM(shape, jnp.bfloat16)] * 5
    summed = pl.pallas_call(
        functools.partial(line_sum_kernel, count),
        out_shape=jax.ShapeDtypeStruct(shape, jnp.bfloat16),
        in_specs=[pl.BlockSpec(memory_space=pltpu.VMEM)],
        out_specs=pl.BlockSpec(memory_space=pltpu.VMEM),
        scratch_shapes=scratch + [pltpu.SemaphoreType.DMA((8, streams, count))],
        compiler_params=pltpu.CompilerParams(collective_id=ident, has_side_effects=True),
        name="line_sum",
    )(values.reshape(shape))
    return jnp.split(summed.reshape(rows, width), len(parts), axis=0)


def pack_small(small, rows):
    columns = -(-small.shape[-1] // rows)
    padded = -(-columns // LANES) * LANES
    lead = small.shape[:-1]
    pads = [(0, 0)] * len(lead)
    filled = jnp.pad(small, pads + [(0, rows * columns - small.shape[-1])])
    filled = filled.reshape(lead + (rows, columns))
    return jnp.pad(filled, pads + [(0, 0), (0, padded - columns)])


def unpack_small(block, rows, size):
    columns = -(-size // rows)
    return block[:, :columns].reshape(-1, rows * columns)[:, :size]


def per_device(
    tokens,
    segments,
    projections,
    offsets,
    mixing,
    upward,
    thresholds,
    downward,
    scales,
    shifts,
    biases,
    cotangent,
):
    micro, block_len, width = tokens.shape
    seq_len = segments.shape[1]
    shards = lax.axis_size(SHARDS)
    heads = offsets.shape[1]
    piece = offsets.shape[2]
    head_size = piece * shards
    inner = heads * head_size
    rows = upward.shape[0]
    hidden_units = upward.shape[1]
    start = lax.axis_index("seq") * block_len
    query_pos = start + jnp.arange(block_len, dtype=jnp.int32)
    key_pos = jnp.arange(seq_len, dtype=jnp.int32)

    small = jnp.concatenate(
        [
            offsets.reshape(-1),
            thresholds.reshape(-1),
            scales.reshape(-1),
            shifts.reshape(-1),
            biases.reshape(-1),
        ]
    )
    small_size = small.shape[0]
    packed = jnp.concatenate(
        [
            mixing.T,
            projections[0],
            projections[1],
            projections[2],
            pack_small(small, rows),
        ],
        axis=1,
    )
    full = lax.all_gather(packed, SHARDS, axis=0, tiled=True)
    mix_t = full[:, :inner]
    entry = full[:, inner : 4 * inner]
    table = unpack_small(full[:, 4 * inner :], rows, small_size)
    table = table.astype(jnp.float32)
    cuts = [0, offsets.size, offsets.size + thresholds.size]
    offset_rows = (
        table[:, cuts[0] : cuts[1]]
        .reshape(shards, 2, heads, piece)
        .transpose(1, 2, 0, 3)
        .reshape(2, inner)
    )
    threshold_row = (
        table[:, cuts[1] : cuts[2]]
        .reshape(shards, thresholds.shape[0], thresholds.shape[1])
        .transpose(1, 0, 2)
        .reshape(-1)
    )
    norm_rows = (
        table[:, cuts[2] :].reshape(shards, 6, rows).transpose(1, 0, 2).reshape(6, shards * rows)
    )
    scale_rows, shift_rows, bias_rows = norm_rows[0:2], norm_rows[2:4], norm_rows[4:6]

    inputs = []
    normals = []
    inverses = []
    normed = []
    stacks = []
    for b in range(micro):
        value = tokens[b].astype(jnp.float32)
        normal, inverse = norm_stats(value)
        inputs.append(value)
        normals.append(normal)
        inverses.append(inverse)
        normed.append((normal * scale_rows[0] + shift_rows[0]).astype(jnp.bfloat16))
        stacks.append(dot("cd,de->ce", normed[b], entry))
    query_b = [(s[:, :inner] + offset_rows[0]).astype(jnp.bfloat16) for s in stacks]
    key_value = jnp.stack(
        [
            jnp.concatenate(
                [s[:, inner : 2 * inner], s[:, 2 * inner :] + offset_rows[1]], axis=1
            ).astype(jnp.bfloat16)
            for s in stacks
        ]
    )
    key_value_full = lax.all_gather(key_value, "seq", axis=1, tiled=True)
    packed_ffn = jnp.concatenate([upward, downward.T], axis=1)
    packed_ffn, key_value_full = lax.optimization_barrier((packed_ffn, key_value_full))
    full_ffn = lax.all_gather(packed_ffn, SHARDS, axis=0, tiled=True)
    up = full_ffn[:, :hidden_units]
    down_t = full_ffn[:, hidden_units:]

    allowed = []
    probs_all = []
    attended = []
    branch = []
    for b in range(micro):
        seg_row = segments[b]
        own_seg = lax.dynamic_slice_in_dim(seg_row, start, block_len)
        allowed.append(
            (key_pos[None, :] <= query_pos[:, None]) & (seg_row[None, :] == own_seg[:, None])
        )
        pieces = []
        totals = []
        for h in range(heads):
            cols = slice(h * head_size, (h + 1) * head_size)
            vcols = slice(inner + h * head_size, inner + (h + 1) * head_size)
            scores = head_scores(query_b[b][:, cols], key_value_full[b][:, cols], allowed[b])
            log_total = jax.nn.logsumexp(scores, axis=1, keepdims=True)
            weights_b = jnp.exp(scores - log_total).astype(jnp.bfloat16)
            pieces.append(dot("qk,ke->qe", weights_b, key_value_full[b][:, vcols]))
            totals.append(log_total)
        probs_all.append(totals)
        attended.append(jnp.concatenate(pieces, axis=1).astype(jnp.bfloat16))
        branch.append(dot("ce,de->cd", attended[b], mix_t))

    branch = tensor_sum(branch, 8, 0)
    hidden = []
    normals2 = []
    inverses2 = []
    normed2 = []
    pre_act = []
    activated = []
    lifted = []
    for b in range(micro):
        hidden.append(inputs[b] + branch[b].astype(jnp.float32) + bias_rows[0])
        normal, inverse = norm_stats(hidden[b])
        normals2.append(normal)
        inverses2.append(inverse)
        normed2.append((normal * scale_rows[1] + shift_rows[1]).astype(jnp.bfloat16))
        pre_act.append(dot("cd,df->cf", normed2[b], up) + threshold_row)
        activated.append(gelu_tanh(pre_act[b]).astype(jnp.bfloat16))

    grad_pre = []
    grad_sum2 = []
    for b in range(micro):
        grad_act = dot("cd,df->cf", cotangent[b], down_t)
        unused, gelu_back = jax.vjp(gelu_tanh, pre_act[b])
        grad_pre.append(gelu_back(grad_act)[0].astype(jnp.bfloat16))
        grad_sum2.append(dot("cf,df->cd", grad_pre[b], up))
    for b in range(micro):
        lifted.append(dot("cf,df->cd", activated[b], down_t))
    sums = tensor_sum(grad_sum2 + lifted, 16, 1)
    grad_sum2, lifted = sums[:micro], sums[micro:]
    results = [
        (hidden[b] + lifted[b].astype(jnp.float32) + bias_rows[1]).astype(jnp.bfloat16)
        for b in range(micro)
    ]

    both = lambda parts: jnp.concatenate(parts, axis=0)
    grad_pre_all = both(grad_pre)
    cotangent_all = cotangent.reshape(micro * block_len, width)
    threshold_grad = jnp.sum(grad_pre_all.astype(jnp.float32), axis=0)
    ffn_grads = jnp.concatenate(
        [
            dot("cd,cf->df", both(normed2), grad_pre_all).astype(jnp.bfloat16),
            dot("cd,cf->df", cotangent_all, both(activated)).astype(jnp.bfloat16),
        ],
        axis=1,
    )
    ffn_own = lax.psum_scatter(ffn_grads, SHARDS, scatter_dimension=0, tiled=True)

    grad_hidden = []
    grad_hidden_b = []
    scale2 = 0.0
    shift2 = 0.0
    query_grads = []
    key_value_grads = []
    for b in range(micro):
        grad_norm2 = grad_sum2[b].astype(jnp.float32)
        grad_hidden.append(
            cotangent[b].astype(jnp.float32)
            + norm_back(normals2[b], inverses2[b], scale_rows[1], grad_norm2)
        )
        scale2 += jnp.sum(grad_norm2 * normals2[b], axis=0)
        shift2 += jnp.sum(grad_norm2, axis=0)
        grad_hidden_b.append(grad_hidden[b].astype(jnp.bfloat16))
        grad_attended = dot("cd,de->ce", grad_hidden_b[b], mix_t).astype(jnp.bfloat16)
        grads_q = []
        grads_k = []
        grads_v = []
        for h in range(heads):
            cols = slice(h * head_size, (h + 1) * head_size)
            vcols = slice(inner + h * head_size, inner + (h + 1) * head_size)
            scores = head_scores(query_b[b][:, cols], key_value_full[b][:, cols], allowed[b])
            probs = jnp.exp(scores - probs_all[b][h])
            grad_slice = grad_attended[:, cols]
            grad_probs = dot("qe,ke->qk", grad_slice, key_value_full[b][:, vcols])
            delta = jnp.sum(probs * grad_probs, axis=1, keepdims=True)
            grad_scores = (probs * (grad_probs - delta)).astype(jnp.bfloat16)
            grads_q.append(dot("qk,ke->qe", grad_scores, key_value_full[b][:, cols]) * 0.125)
            grads_v.append(dot("qk,qe->ke", probs.astype(jnp.bfloat16), grad_slice))
            grads_k.append(dot("qk,qe->ke", grad_scores, query_b[b][:, cols]) * 0.125)
        query_grads.append(jnp.concatenate(grads_q, axis=1).astype(jnp.bfloat16))
        key_value_grads.append(jnp.concatenate(grads_k + grads_v, axis=1).astype(jnp.bfloat16))
    key_value_own = lax.psum_scatter(
        jnp.stack(key_value_grads), "seq", scatter_dimension=1, tiled=True
    )

    triples = []
    grad_normed = []
    for b in range(micro):
        triples.append(jnp.concatenate([query_grads[b], key_value_own[b]], axis=1))
        grad_normed.append(dot("ce,de->cd", triples[b], entry))
    grad_normed = tensor_sum(grad_normed, 8, 0)
    triple_all = both(triples)
    grad_hidden_all = both(grad_hidden_b)
    triple_sums = jnp.sum(triple_all.astype(jnp.float32), axis=0)
    scale1 = 0.0
    shift1 = 0.0
    bias1 = 0.0
    input_grads = []
    for b in range(micro):
        grad_norm = grad_normed[b].astype(jnp.float32)
        back = norm_back(normals[b], inverses[b], scale_rows[0], grad_norm)
        input_grads.append((grad_hidden[b] + back).astype(jnp.bfloat16))
        scale1 += jnp.sum(grad_norm * normals[b], axis=0)
        shift1 += jnp.sum(grad_norm, axis=0)
        bias1 += jnp.sum(grad_hidden[b], axis=0)
    bias2 = jnp.sum(cotangent_all.astype(jnp.float32), axis=0)

    offset_grad = jnp.stack([triple_sums[:inner], triple_sums[2 * inner :]])
    small_grads = jnp.concatenate(
        [
            offset_grad.reshape(2, heads, shards, piece).transpose(2, 0, 1, 3).reshape(shards, -1),
            threshold_grad.reshape(thresholds.shape[0], shards, thresholds.shape[1])
            .transpose(1, 0, 2)
            .reshape(shards, -1),
            jnp.stack([scale1, scale2, shift1, shift2, bias1, bias2])
            .reshape(6, shards, rows)
            .transpose(1, 0, 2)
            .reshape(shards, -1),
        ],
        axis=1,
    )
    small_block = pack_small(small_grads, rows).reshape(shards * rows, -1)
    att_grads = jnp.concatenate(
        [
            dot("cd,ce->de", grad_hidden_all, both(attended)).astype(jnp.bfloat16),
            dot("cd,ce->de", both(normed), triple_all).astype(jnp.bfloat16),
            small_block.astype(jnp.bfloat16),
        ],
        axis=1,
    )
    att_own = lax.psum_scatter(att_grads, SHARDS, scatter_dimension=0, tiled=True)
    att_own = att_own.astype(jnp.float32)
    ffn_own = ffn_own.astype(jnp.float32)
    own_small = unpack_small(att_own[:, 4 * inner :], rows, small_size)[0]
    own_norms = own_small[cuts[2] :].reshape(6, rows)
    own_entry = att_own[:, inner : 4 * inner]
    return (
        jnp.stack(results),
        jnp.stack(input_grads),
        jnp.stack([own_entry[:, t * inner : (t + 1) * inner] for t in range(3)]),
        own_small[cuts[0] : cuts[1]].reshape(offsets.shape),
        att_own[:, :inner].T,
        ffn_own[:, :hidden_units],
        own_small[cuts[1] : cuts[2]].reshape(thresholds.shape),
        ffn_own[:, hidden_units:].T,
        own_norms[0:2],
        own_norms[2:4],
        own_norms[4:6],
    )


def solution(mesh):
    placed = (
        P("dp", "seq", None),
        P("dp", None),
        P(None, ("dp", "seq"), "tensor"),
        P(None, "tensor", ("dp", "seq")),
        P("tensor", ("dp", "seq")),
        P(("dp", "seq"), "tensor"),
        P("tensor", ("dp", "seq")),
        P("tensor", ("dp", "seq")),
        P(None, ("dp", "seq")),
        P(None, ("dp", "seq")),
        P(None, ("dp", "seq")),
        P("dp", "seq", None),
    )
    return jax.shard_map(
        per_device,
        mesh=mesh,
        in_specs=placed,
        out_specs=(
            P("dp", "seq", None),
            P("dp", "seq", None),
            P(None, ("dp", "seq"), "tensor"),
            P(None, "tensor", ("dp", "seq")),
            P("tensor", ("dp", "seq")),
            P(("dp", "seq"), "tensor"),
            P("tensor", ("dp", "seq")),
            P("tensor", ("dp", "seq")),
            P(None, ("dp", "seq")),
            P(None, ("dp", "seq")),
            P(None, ("dp", "seq")),
        ),
        check_vma=False,
    )
```
